32 devices in a mesh: stack: 2 (over y), acq: 4 (over z), lines: 4 (over x, core).
Axes of the slice: x: 2, y: 2, z: 4, core: 2. Of those that a mesh axis runs over, the one named last changes fastest.
Arguments:
- returned_radar_signal_data: bfloat16 [8, 2, 512, 4096], P(('stack', 'acq'), None, 'lines'), parts along dimension 0, may hold values from -6 to 6
- slant_replica_filter_response: float32 [8, 2, 4096], P(('stack', 'acq')), parts along dimension 0, may hold values from -6 to 6
- along_track_sharpening_slope: float32 [8, 4096], P(('stack', 'acq'), 'lines'), parts along dimension 0, may hold values from 0.25 to 1
- motion_shift_centroid_hz: float32 [8, 4096], P(('stack', 'acq'), 'lines'), parts along dimension 0, may hold values from -0.2 to 0.2
- valid_along_track_rows: int32 [8], P(('stack', 'acq')), parts along dimension 0, may hold values from 256 to 512, as said below
- reference_index: int32 [2], P('stack'), parts along dimension 0, may hold values from 0 to 3
- patch_offsets: int32 [8, 2, 4, 32], P(('stack', 'acq'), None, None, 'lines'), parts along dimension 0, may hold values from -64 to 64
Outputs:
- correlation: float32 [8, 2, 256, 2048], P(('stack', 'acq'), None, None, 'lines'), parts along dimension 0
The draws below stay inside these ranges and needn't reach their ends.
There are 2 independent parts, one for each index of `stack`. The reference program is written for one: setup_inputs(seed, part) draws one part's arguments, and reference() takes and returns one part's arrays. A program takes and returns all parts, laid end to end along the dimension named above; each array names one. Nothing has to cross between parts.
Inputs may be any that keep to these rules, and one draw needn't show every extreme that they name: `valid_along_track_rows`: some acquisition has all 512 lines valid and some exactly half of them.
All inputs are finite; a program needn't handle non-finite values.
Results may differ from the reference program's by a relative error of at most 0.0053.
Values may be sent and summed in bfloat16 or wider, within the bound.
A program may use at most 64 MiB of HBM per device.

```python
import math
import jax
import jax.numpy as jnp
from jax import lax

NA = 512
NR = 4096
PATCH = 64
ACQ = 4


def draw_valid_along_track_rows(key, part):
    counts = jax.random.randint(jax.random.fold_in(key, 11), (ACQ,), NA // 2, NA + 1)
    order = jax.random.permutation(jax.random.fold_in(key, 12), ACQ)
    counts = jnp.where(order == 0, NA, counts)
    counts = jnp.where(order == 1, NA // 2, counts)
    return counts.astype(jnp.int32)


def set_ends(array, own_key, least, top_value):
    longest = array.shape.index(max(array.shape))
    spots = []
    for shift in (0, 1):
        where = [jax.random.randint(jax.random.fold_in(own_key, axis), (), 0, length) for axis, length in enumerate(array.shape)]
        where[longest] = (where[longest] + shift) % array.shape[longest]
        spots.append(tuple(where))
    return array.at[spots[0]].set(least).at[spots[1]].set(top_value)


def block_scale(own_key, extent, pieces, least, high):
    gain, own = 1.0, jax.random.fold_in(own_key, 6)
    for axis_at, shards_of in pieces:
        draws = jnp.exp(jax.random.uniform(jax.random.fold_in(own, axis_at), (shards_of,), jnp.float32, least / len(pieces), high / len(pieces)))
        gain = gain * jnp.repeat(draws, extent[axis_at] // shards_of).reshape([-1 if axis == axis_at else 1 for axis in range(len(extent))])
    return gain


def bell_draw(own_key, shape, deviation, reach, shards=(), kind=jnp.bfloat16):
    level = block_scale(own_key, shape, shards, -0.22, 0.18) if shards else 1.0
    result = jax.random.normal(own_key, shape, jnp.float32) * deviation * level
    return jnp.minimum(jnp.maximum(result, -reach), reach).astype(kind)


def setup_inputs(seed: int = 0, part: int = 0) -> dict:
    key_list = jax.random.split(jax.random.key(seed), 8)
    own_keys = jax.random.split(jax.random.fold_in(key_list[7], part), 8)
    returned_radar_signal_data = bell_draw(own_keys[0], (ACQ, 2, NA, NR), 0.7, 6.0, ((0, 4), (2, 4)))
    slant_replica_filter_response = bell_draw(own_keys[1], (ACQ, 2, NR), 0.7, 6.0, ((0, 4),), jnp.float32)
    along_track_sharpening_slope = jnp.clip(jnp.exp(math.log(1.0) - 1.3862944 * jax.random.uniform(own_keys[2], (ACQ, NR), jnp.float32) ** block_scale(own_keys[2], (ACQ, NR), ((0, 4), (1, 4)), -0.2, 0.2)), 0.25, 1.0)
    motion_shift_centroid_hz = jnp.clip(jax.random.uniform(own_keys[3], (ACQ, NR), jnp.float32, -0.2, 0.2) * block_scale(own_keys[3], (ACQ, NR), ((0, 4), (1, 4)), -0.4, 0.0), -0.2, 0.2)
    valid_along_track_rows = draw_valid_along_track_rows(jax.random.fold_in(jax.random.fold_in(key_list[7], part), 71), part)
    reference_index = jax.random.randint(own_keys[5], (1,), 0, ACQ).astype(jnp.int32)
    patch_offsets = set_ends(jax.random.randint(own_keys[6], (ACQ, 2, NA // (2 * PATCH), NR // (2 * PATCH)), -PATCH, PATCH + 1), jax.random.fold_in(own_keys[6], 1), -PATCH, PATCH).astype(jnp.int32)
    return {"returned_radar_signal_data": returned_radar_signal_data, "slant_replica_filter_response": slant_replica_filter_response, "along_track_sharpening_slope": along_track_sharpening_slope, "motion_shift_centroid_hz": motion_shift_centroid_hz, "valid_along_track_rows": valid_along_track_rows, "reference_index": reference_index, "patch_offsets": patch_offsets}


eps = 1e-06

def sharpen_one_pulse_group(vectorized_inputs):
    raw_one, filter_one, rate_one, centre_one, valid_one = vectorized_inputs
    line_index = jnp.arange(NA, dtype=jnp.int32)[:, None]
    keep_mask = (line_index < valid_one).astype(jnp.float32)
    echo = lax.complex(raw_one[0].astype(jnp.float32) * keep_mask, raw_one[1].astype(jnp.float32) * keep_mask)
    spectrum = jnp.fft.fft(echo, axis=1) * lax.complex(filter_one[0], filter_one[1])[None, :]
    compressed = jnp.fft.ifft(spectrum, axis=1)
    real_part = lax.optimization_barrier(jnp.real(compressed).astype(jnp.bfloat16)).astype(jnp.float32)
    imaginary = lax.optimization_barrier(jnp.imag(compressed).astype(jnp.bfloat16)).astype(jnp.float32)
    along = jnp.fft.fft(lax.complex(real_part, imaginary), axis=0)
    freq_index = jnp.arange(NA, dtype=jnp.int32)
    signed_freq = jnp.where(freq_index >= NA // 2, freq_index - NA, freq_index).astype(jnp.float32) / NA
    offset_freq = signed_freq[:, None] - centre_one[None, :]
    phase_angle = math.pi * NA / 4.0 * rate_one[None, :] * offset_freq * offset_freq
    along = along * lax.complex(jnp.cos(phase_angle), jnp.sin(phase_angle))
    focused = jnp.fft.ifft(along, axis=0)
    return jnp.stack([jnp.real(focused), jnp.imag(focused)]).astype(jnp.bfloat16)

def reference(returned_radar_signal_data, slant_replica_filter_response, along_track_sharpening_slope, motion_shift_centroid_hz, valid_along_track_rows, reference_index, patch_offsets):
    sharpened_acquisition_pictures = lax.map(sharpen_one_pulse_group, (returned_radar_signal_data, slant_replica_filter_response, along_track_sharpening_slope, motion_shift_centroid_hz, valid_along_track_rows))
    primary_image = sharpened_acquisition_pictures[reference_index[0]].astype(jnp.float32)
    row_blocks = NA // (2 * PATCH)
    col_blocks = NR // (2 * PATCH)
    half = PATCH // 2
    blocks = primary_image.reshape(2, row_blocks, 2 * PATCH, col_blocks, 2 * PATCH)
    blocks = blocks[:, :, half:half + PATCH, :, half:half + PATCH]
    blocks = blocks.transpose(1, 3, 0, 2, 4).reshape(row_blocks * col_blocks, 2, PATCH, PATCH)
    primary_stack = lax.complex(blocks[:, 0], blocks[:, 1])
    primary_power = lax.optimization_barrier(jnp.mean(blocks[:, 0] * blocks[:, 0] + blocks[:, 1] * blocks[:, 1], axis=(1, 2)))
    primary_spectrum = jnp.fft.fft2(primary_stack)
    block_row = lax.broadcasted_iota(jnp.int32, (row_blocks, col_blocks), 0)
    block_col = lax.broadcasted_iota(jnp.int32, (row_blocks, col_blocks), 1)

    def correlate(vectorized_inputs):
        image, offsets = vectorized_inputs
        padded = jnp.pad(image.astype(jnp.float32), ((0, 0), (half, half), (half, half)))
        row_start = (2 * PATCH * block_row + PATCH + offsets[0]).reshape(-1)
        col_start = (2 * PATCH * block_col + PATCH + offsets[1]).reshape(-1)

        def window(start_row, start_col):
            zero = jnp.zeros((), jnp.int32)
            return lax.dynamic_slice(padded, (zero, start_row, start_col), (2, PATCH, PATCH))
        second_stack = jax.vmap(window)(row_start, col_start)
        second_power = lax.optimization_barrier(jnp.mean(second_stack[:, 0] * second_stack[:, 0] + second_stack[:, 1] * second_stack[:, 1], axis=(1, 2)))
        second_spectrum = jnp.fft.fft2(lax.complex(second_stack[:, 0], second_stack[:, 1]))
        surface = jnp.fft.ifft2(primary_spectrum * jnp.conj(second_spectrum))
        scale = 1.0 / (PATCH * jnp.sqrt(primary_power + eps) * jnp.sqrt(second_power + eps))
        surface = surface * scale[:, None, None]
        stacked = jnp.stack([jnp.real(surface), jnp.imag(surface)]).astype(jnp.float32)
        stacked = stacked.reshape(2, row_blocks, col_blocks, PATCH, PATCH).transpose(0, 1, 3, 2, 4)
        return stacked.reshape(2, row_blocks * PATCH, col_blocks * PATCH)
    return lax.map(correlate, (sharpened_acquisition_pictures, patch_offsets))
```

```python
import functools
import math

import jax
import jax.numpy as jnp
import numpy as np
from jax import lax
from jax.experimental import pallas as pl
from jax.experimental.pallas import tpu as pltpu
from jax.sharding import PartitionSpec as P

PATCH = 64
LANES = 128
eps = 1e-06
bf16 = jnp.bfloat16
f32 = jnp.float32


def dft(size, sign):
    index = np.arange(size)
    angle = 2.0 * np.pi * (np.outer(index, index) % size) / size
    return np.cos(angle) + 1j * sign * np.sin(angle)


def right_form(matrix):
    return np.block([[matrix.real, matrix.imag], [-matrix.imag, matrix.real]])


def left_form(matrix):
    return np.block([[matrix.real, -matrix.imag], [matrix.imag, matrix.real]])


def halves(matrix):
    high = np.asarray(matrix, np.float32).astype(bf16)
    low = (np.asarray(matrix, np.float64) - high.astype(np.float64)).astype(bf16)
    return np.stack([high, low])


def split(value):
    high = value.astype(bf16)
    return high, (value - high.astype(f32)).astype(bf16)


def dot(a, b):
    return jnp.dot(a, b, preferred_element_type=f32)


def fft_list(values, sign):
    count = len(values)
    if count == 1:
        return values
    even = fft_list(values[0::2], sign)
    odd = fft_list(values[1::2], sign)
    out = [None] * count
    for k in range(count // 2):
        re, im = odd[k]
        if k == 0:
            pass
        elif 4 * k == count:
            re, im = (-im, re) if sign > 0 else (im, -re)
        elif 8 * k == count:
            r = math.sqrt(0.5)
            re, im = ((re - im) * r, (re + im) * r) if sign > 0 else ((re + im) * r, (im - re) * r)
        elif 8 * k == 3 * count:
            r = math.sqrt(0.5)
            re, im = ((re + im) * -r, (re - im) * r) if sign > 0 else ((im - re) * r, (re + im) * -r)
        else:
            c = math.cos(2 * math.pi * k / count)
            s = sign * math.sin(2 * math.pi * k / count)
            re, im = re * c - im * s, re * s + im * c
        out[k] = (even[k][0] + re, even[k][1] + im)
        out[k + count // 2] = (even[k][0] - re, even[k][1] - im)
    return out


def range_body(valid_ref, echo_ref, filt_ref, tw_ref, fwd_ref, inv_ref, out_ref, zh, zl):
    rows = echo_ref.shape[2]
    lead = echo_ref.shape[3] // LANES
    first = lax.axis_index("lines") * (rows * pl.num_programs(0)) + pl.program_id(0) * rows
    group = 16

    def load(g):
        r0 = g * group
        line = first + r0 + lax.broadcasted_iota(jnp.int32, (group, 1), 0)
        keep = (line < valid_ref[0]).astype(f32)
        values = [
            tuple(
                echo_ref[0, q, r0 : r0 + group, LANES * a : LANES * a + LANES].astype(f32) * keep
                for q in range(2)
            )
            for a in range(lead)
        ]
        for c, (re, im) in enumerate(fft_list(values, -1.0)):
            tr, ti = tw_ref[0, c : c + 1, :], tw_ref[1, c : c + 1, :]
            put(c * rows + r0, group, re * tr - im * ti, re * ti + im * tr)

    def put(row, count, re, im):
        zh[row : row + count, :LANES], zl[row : row + count, :LANES] = split(re)
        zh[row : row + count, LANES:], zl[row : row + count, LANES:] = split(im)

    def product(m_ref):
        h = zh[...]
        return dot(h, m_ref[0]) + dot(zl[...], m_ref[0]) + dot(h, m_ref[1])

    for g in range(rows // group):
        load(g)
    y = product(fwd_ref)
    for c in range(lead):
        part = y[c * rows : c * rows + rows]
        re, im = part[:, :LANES], part[:, LANES:]
        hr, hi = filt_ref[0, c : c + 1, :], filt_ref[1, c : c + 1, :]
        put(c * rows, rows, re * hr - im * hi, re * hi + im * hr)
    y = product(inv_ref)
    for g in range(rows // group):
        r0 = g * group
        values = []
        for c in range(lead):
            part = y[c * rows + r0 : c * rows + r0 + group]
            re, im = part[:, :LANES], part[:, LANES:]
            tr, ti = tw_ref[0, c : c + 1, :], tw_ref[1, c : c + 1, :]
            values.append((re * tr + im * ti, im * tr - re * ti))
        for a, pair in enumerate(fft_list(values, 1.0)):
            for q in range(2):
                out_ref[q, r0 : r0 + group, LANES * a : LANES * a + LANES] = pair[q].astype(bf16)


def range_compress(valid, echo, filt):
    rows, length = echo.shape[2:]
    lead = length // LANES
    block = min(rows, 32)
    fwd = halves(right_form(dft(LANES, -1.0)))
    inv = halves(right_form(dft(LANES, 1.0)))
    angle = 2 * np.pi * np.outer(np.arange(lead), np.arange(LANES)) / length
    tw = np.stack([np.cos(angle), -np.sin(angle)]).astype(np.float32)
    filt = filt[0].reshape(2, LANES, lead).transpose(0, 2, 1) * (1.0 / length)
    whole = lambda x: pl.BlockSpec(x.shape, lambda g: (0,) * x.ndim)
    return pl.pallas_call(
        range_body,
        grid=(rows // block,),
        in_specs=[
            pl.BlockSpec(memory_space=pltpu.SMEM),
            pl.BlockSpec((1, 2, block, length), lambda g: (0, 0, g, 0)),
            whole(filt),
            whole(tw),
            whole(fwd),
            whole(inv),
        ],
        out_specs=pl.BlockSpec((2, block, length), lambda g: (0, g, 0)),
        out_shape=jax.ShapeDtypeStruct((2, rows, length), bf16),
        scratch_shapes=[pltpu.VMEM((lead * block, 2 * LANES), bf16)] * 2,
        name="range_compress",
    )(valid, echo, filt, tw, fwd, inv)


def unit_polys():
    z = 0.125 - 0.125 * np.cos(np.pi * (np.arange(400) + 0.5) / 400)
    f = np.sqrt(z)
    cosine = np.polynomial.Polynomial.fit(z, np.cos(2 * np.pi * f), 7, domain=[0, 0.25]).convert()
    sine = np.polynomial.Polynomial.fit(z, np.sin(2 * np.pi * f) / f, 6, domain=[0, 0.25]).convert()
    return [float(v) for v in cosine.coef], [float(v) for v in sine.coef]


def cos_sin_turns(turns):
    cosine, sine = unit_polys()
    frac = turns - jnp.round(turns)
    z = frac * frac

    def horner(coef):
        value = jnp.full_like(z, coef[-1])
        for v in coef[-2::-1]:
            value = value * z + v
        return value

    return horner(cosine), horner(sine) * frac


def azimuth_body(in_ref, slope_ref, centre_ref, fwd_ref, inv_ref, sel_ref, out_ref, crop_ref):
    total, cols = in_ref.shape[1:]
    lead = total // LANES
    values = [
        tuple(in_ref[q, LANES * a : LANES * a + LANES, :].astype(f32) for q in range(2))
        for a in range(lead)
    ]
    values = fft_list(values, -1.0)
    sharp = slope_ref[...] * (total / 8.0)
    centre = centre_ref[...]
    back = []
    for c in range(lead):
        h, l = split(jnp.concatenate(values[c], axis=0))
        y = dot(fwd_ref[0, c], h) + dot(fwd_ref[0, c], l) + dot(fwd_ref[1, c], h)
        k = c + lead * lax.broadcasted_iota(jnp.int32, (LANES, 1), 0)
        u = jnp.where(k >= total // 2, k - total, k).astype(f32) * (1.0 / total)
        w = u - centre
        co, si = cos_sin_turns(sharp * w * w)
        re, im = y[:LANES], y[LANES:]
        h, l = split(jnp.concatenate([re * co - im * si, re * si + im * co], axis=0))
        y = dot(inv_ref[0, c], h) + dot(inv_ref[0, c], l) + dot(inv_ref[1, c], h)
        back.append((y[:LANES], y[LANES:]))
    half = PATCH // 2
    for a, pair in enumerate(fft_list(back, 1.0)):
        for q in range(2):
            image = pair[q].astype(bf16)
            out_ref[q, LANES * a : LANES * a + LANES, :] = image
            crop = dot(image[half : half + PATCH], sel_ref[...])
            crop_ref[q, PATCH * a : PATCH * a + PATCH, :] = crop.astype(bf16)


def azimuth_focus(turned, slope, centre):
    total, cols = turned.shape[1:]
    lead = total // LANES
    block = 2 * LANES
    fwd, inv = [], []
    for c in range(lead):
        phase = np.exp(-2j * np.pi * c * np.arange(LANES) / total)
        fwd.append(left_form(dft(LANES, -1.0) * phase[None, :]))
        inv.append(left_form(dft(LANES, 1.0) * phase.conj()[:, None] / total))
    fwd, inv = halves(np.stack(fwd)), halves(np.stack(inv))
    sel = np.zeros((block, LANES), np.float32)
    lane = np.arange(PATCH)
    sel[lane + PATCH // 2, lane] = 1
    sel[lane + LANES + PATCH // 2, lane + PATCH] = 1
    sel = sel.astype(bf16)
    whole = lambda x: pl.BlockSpec(x.shape, lambda g: (0,) * x.ndim)
    column = lambda shape: pl.BlockSpec(shape, lambda g: (0,) * (len(shape) - 1) + (g,))
    return pl.pallas_call(
        azimuth_body,
        grid=(cols // block,),
        in_specs=[
            column((2, total, block)),
            column((1, block)),
            column((1, block)),
            whole(fwd),
            whole(inv),
            whole(sel),
        ],
        out_specs=[column((2, total, block)), column((2, total // 2, LANES))],
        out_shape=[
            jax.ShapeDtypeStruct((2, total, cols), bf16),
            jax.ShapeDtypeStruct((2, total // 2, cols // 2), bf16),
        ],
        name="azimuth_focus",
    )(turned, slope, centre, fwd, inv, sel)


def correlate_body(
    off_ref, image_ref, left_ref, right_ref, crop_ref, fr_ref, fl_ref, ir_ref, il_ref, ones_ref,
    out_ref, padded, stack, high, low, power,
):
    total, cols = image_ref.shape[1:]
    half = PATCH // 2
    row_blocks, pairs = total // LANES, cols // (2 * LANES)
    count = row_blocks * pairs
    for q in range(2):
        padded[q, :half, :] = jnp.zeros((half, cols + 3 * LANES), f32)
        padded[q, half + total :, :] = jnp.zeros((half + 8, cols + 3 * LANES), f32)
        padded[q, half : half + total, :LANES] = left_ref[q].astype(f32)
        padded[q, half : half + total, LANES : LANES + cols] = image_ref[q].astype(f32)
        padded[q, half : half + total, LANES + cols : 2 * LANES + cols] = right_ref[q].astype(f32)
    lane = lax.broadcasted_iota(jnp.int32, (1, LANES), 1)

    def window(q, i, j, target):
        row = LANES * i + PATCH + off_ref[0, 0, i, j]
        col = LANES * j + LANES + half + off_ref[0, 1, i, j]
        base = pl.multiple_of(col // LANES * LANES, LANES)
        offset = col - base
        shift = (target - offset + LANES) % LANES
        top = pl.multiple_of(row // 8 * 8, 8)
        first = padded[q, pl.ds(top, PATCH + 8), pl.ds(base, LANES)]
        second = padded[q, pl.ds(top, PATCH + 8), pl.ds(pl.multiple_of(base + LANES, LANES), LANES)]
        first = pltpu.roll(first, shift, 1)
        second = pltpu.roll(second, shift, 1)
        joined = jnp.where(lane + offset - target < LANES, first, second)
        return pltpu.roll(joined, (PATCH + 8 - (row - top)) % (PATCH + 8), 0)[:PATCH]

    def total_of(re, im):
        return jnp.sum(re * re + im * im, axis=0, keepdims=True)

    for i in range(row_blocks):
        for jp in range(pairs):
            n = i * pairs + jp
            parts = [
                jnp.where(lane < PATCH, window(q, i, 2 * jp, 0), window(q, i, 2 * jp + 1, PATCH))
                for q in range(2)
            ]
            power[count + n : count + n + 1, :] = total_of(*parts)
            prime = [
                crop_ref[q, PATCH * i : PATCH * i + PATCH, LANES * jp : LANES * jp + LANES]
                for q in range(2)
            ]
            power[n : n + 1, :] = total_of(prime[0].astype(f32), prime[1].astype(f32))
            for q in range(2):
                stack[PATCH * n : PATCH * n + PATCH, LANES * q : LANES * q + LANES] = prime[q]
                at = PATCH * (count + n)
                stack[at : at + PATCH, LANES * q : LANES * q + LANES] = parts[q].astype(bf16)

    y = dot(stack[...], fr_ref[0]) + dot(stack[...], fr_ref[1])
    for n in range(2 * count):
        part = y[PATCH * n : PATCH * n + PATCH]
        for q in range(2):
            h, l = split(part[:, LANES * q : LANES * q + LANES])
            high[PATCH * q : PATCH * q + PATCH, LANES * n : LANES * n + LANES] = h
            low[PATCH * q : PATCH * q + PATCH, LANES * n : LANES * n + LANES] = l

    def left(m_ref, h, l):
        return dot(m_ref[0], h) + dot(m_ref[0], l) + dot(m_ref[1], h)

    z = left(fl_ref, high[...], low[...])
    wide = count * LANES
    pr, pi, sr, si = z[:PATCH, :wide], z[PATCH:, :wide], z[:PATCH, wide:], z[PATCH:, wide:]
    cross = jnp.concatenate([pr * sr + pi * si, pi * sr - pr * si], axis=0)
    x = left(il_ref, *split(cross))
    for n in range(count):
        for q in range(2):
            h, l = split(x[PATCH * q : PATCH * q + PATCH, LANES * n : LANES * n + LANES])
            stack[PATCH * n : PATCH * n + PATCH, LANES * q : LANES * q + LANES] = h
            at = PATCH * (count + n)
            stack[at : at + PATCH, LANES * q : LANES * q + LANES] = l
    h, l = stack[: PATCH * count], stack[PATCH * count :]
    y = dot(h, ir_ref[0]) + dot(l, ir_ref[0]) + dot(h, ir_ref[1])
    means = jnp.dot(
        power[...], ones_ref[...], precision=lax.Precision.HIGHEST, preferred_element_type=f32
    )
    scale = lax.rsqrt(means + eps)
    factor = scale[:count] * scale[count:] * (1.0 / PATCH**3)
    for i in range(row_blocks):
        for jp in range(pairs):
            n = i * pairs + jp
            part = y[PATCH * n : PATCH * n + PATCH]
            for q in range(2):
                out_ref[
                    0, q, PATCH * i : PATCH * i + PATCH, LANES * jp : LANES * jp + LANES
                ] = part[:, LANES * q : LANES * q + LANES] * factor[n : n + 1, :]


def correlate(offsets, image, left, right, crop):
    total, cols = image.shape[1:]
    count = (total // LANES) * (cols // (2 * LANES))
    two = np.eye(2)
    fr = halves(right_form(np.kron(two, dft(PATCH, -1.0))))
    ir = halves(right_form(np.kron(two, dft(PATCH, 1.0))))
    fl = halves(left_form(dft(PATCH, -1.0)))
    il = halves(left_form(dft(PATCH, 1.0)))
    ones = np.kron(two, np.full((PATCH, PATCH), 1.0 / PATCH**2)).astype(np.float32)
    vmem = pl.BlockSpec(memory_space=pltpu.VMEM)
    return pl.pallas_call(
        correlate_body,
        in_specs=[pl.BlockSpec(memory_space=pltpu.SMEM)] + [vmem] * 9,
        out_specs=vmem,
        out_shape=jax.ShapeDtypeStruct((1, 2, total // 2, cols // 2), f32),
        scratch_shapes=[
            pltpu.VMEM((2, total + PATCH + 8, cols + 3 * LANES), f32),
            pltpu.VMEM((2 * count * PATCH, 2 * LANES), bf16),
            pltpu.VMEM((2 * PATCH, 2 * count * LANES), bf16),
            pltpu.VMEM((2 * PATCH, 2 * count * LANES), bf16),
            pltpu.VMEM((2 * count, LANES), f32),
        ],
        name="correlate",
    )(offsets, image, left, right, crop, fr, fl, ir, il, ones)


def on_device(echo, filt, slope, centre, valid, reference_index, offsets):
    compressed = range_compress(valid, echo, filt)
    turned = lax.all_to_all(compressed, "lines", split_axis=2, concat_axis=1, tiled=True)
    focused, crop = azimuth_focus(turned, slope, centre)
    mine = lax.axis_index("acq") == reference_index[0]
    primary = lax.psum(jnp.where(mine, crop, 0).astype(bf16), "acq")
    half = PATCH // 2
    cols = focused.shape[2]
    devices = lax.axis_size("lines")
    up = [(i, i + 1) for i in range(devices - 1)]
    before = lax.ppermute(focused[:, :, cols - half :], "lines", up)
    after = lax.ppermute(focused[:, :, :half], "lines", [(j, i) for i, j in up])
    left = jnp.pad(before, ((0, 0), (0, 0), (LANES - half, 0)))
    right = jnp.pad(after, ((0, 0), (0, 0), (0, LANES - half)))
    return correlate(offsets, focused, left, right, primary)


def solution(mesh):
    return jax.shard_map(
        on_device,
        mesh=mesh,
        in_specs=(
            P(("stack", "acq"), None, "lines", None),
            P(("stack", "acq"), None, None),
            P(("stack", "acq"), "lines"),
            P(("stack", "acq"), "lines"),
            P(("stack", "acq")),
            P("stack"),
            P(("stack", "acq"), None, None, "lines"),
        ),
        out_specs=P(("stack", "acq"), None, None, "lines"),
        check_vma=False,
    )
```

```python
import functools
import math

import jax
import jax.numpy as jnp
import numpy as np
from jax import lax
from jax.experimental import pallas as pl
from jax.experimental.pallas import tpu as pltpu
from jax.sharding import PartitionSpec as P

PATCH = 64
LANES = 128
eps = 1e-06
bf16 = jnp.bfloat16
f32 = jnp.float32


def dft(size, sign):
    index = np.arange(size)
    angle = 2.0 * np.pi * (np.outer(index, index) % size) / size
    return np.cos(angle) + 1j * sign * np.sin(angle)


def right_form(matrix):
    return np.block([[matrix.real, matrix.imag], [-matrix.imag, matrix.real]])


def left_form(matrix):
    return np.block([[matrix.real, -matrix.imag], [matrix.imag, matrix.real]])


def halves(matrix):
    high = np.asarray(matrix, np.float32).astype(bf16)
    low = (np.asarray(matrix, np.float64) - high.astype(np.float64)).astype(bf16)
    return np.stack([high, low])


def split(value):
    high = value.astype(bf16)
    return high, (value - high.astype(f32)).astype(bf16)


def dot(a, b):
    return jnp.dot(a, b, preferred_element_type=f32)


def fft_list(values, sign):
    count = len(values)
    if count == 1:
        return values
    even = fft_list(values[0::2], sign)
    odd = fft_list(values[1::2], sign)
    out = [None] * count
    for k in range(count // 2):
        re, im = odd[k]
        if k == 0:
            pass
        elif 4 * k == count:
            re, im = (-im, re) if sign > 0 else (im, -re)
        elif 8 * k == count:
            r = math.sqrt(0.5)
            re, im = ((re - im) * r, (re + im) * r) if sign > 0 else ((re + im) * r, (im - re) * r)
        elif 8 * k == 3 * count:
            r = math.sqrt(0.5)
            re, im = ((re + im) * -r, (re - im) * r) if sign > 0 else ((im - re) * r, (re + im) * -r)
        else:
            c = math.cos(2 * math.pi * k / count)
            s = sign * math.sin(2 * math.pi * k / count)
            re, im = re * c - im * s, re * s + im * c
        out[k] = (even[k][0] + re, even[k][1] + im)
        out[k + count // 2] = (even[k][0] - re, even[k][1] - im)
    return out


def range_block(r0, block, first, valid, echo_ref, filt_ref, tw_ref, fwd_ref, inv_ref, out_ref, zh, zl):
    lead = echo_ref.shape[3] // LANES
    group = 16

    def put(row, count, re, im):
        zh[row : row + count, :LANES], zl[row : row + count, :LANES] = split(re)
        zh[row : row + count, LANES:], zl[row : row + count, LANES:] = split(im)

    def product(m_ref):
        h = zh[...]
        return dot(h, m_ref[0]) + dot(zl[...], m_ref[0]) + dot(h, m_ref[1])

    for g in range(block // group):
        at = pl.multiple_of(r0 + g * group, group)
        line = first + at + lax.broadcasted_iota(jnp.int32, (group, 1), 0)
        keep = (line < valid).astype(f32)
        values = [
            tuple(
                echo_ref[0, q, pl.ds(at, group), LANES * a : LANES * a + LANES].astype(f32) * keep
                for q in range(2)
            )
            for a in range(lead)
        ]
        for c, (re, im) in enumerate(fft_list(values, -1.0)):
            tr, ti = tw_ref[0, c : c + 1, :], tw_ref[1, c : c + 1, :]
            put(c * block + g * group, group, re * tr - im * ti, re * ti + im * tr)
    y = product(fwd_ref)
    for c in range(lead):
        part = y[c * block : c * block + block]
        re, im = part[:, :LANES], part[:, LANES:]
        hr, hi = filt_ref[0, c : c + 1, :], filt_ref[1, c : c + 1, :]
        put(c * block, block, re * hr - im * hi, re * hi + im * hr)
    y = product(inv_ref)
    for g in range(block // group):
        at = pl.multiple_of(r0 + g * group, group)
        values = []
        for c in range(lead):
            part = y[c * block + g * group : c * block + g * group + group]
            re, im = part[:, :LANES], part[:, LANES:]
            tr, ti = tw_ref[0, c : c + 1, :], tw_ref[1, c : c + 1, :]
            values.append((re * tr + im * ti, im * tr - re * ti))
        for a, pair in enumerate(fft_list(values, 1.0)):
            for q in range(2):
                out_ref[q, pl.ds(at, group), LANES * a : LANES * a + LANES] = pair[q].astype(bf16)


def unit_polys():
    z = 0.125 - 0.125 * np.cos(np.pi * (np.arange(400) + 0.5) / 400)
    f = np.sqrt(z)
    cosine = np.polynomial.Polynomial.fit(z, np.cos(2 * np.pi * f), 7, domain=[0, 0.25]).convert()
    sine = np.polynomial.Polynomial.fit(z, np.sin(2 * np.pi * f) / f, 6, domain=[0, 0.25]).convert()
    return [float(v) for v in cosine.coef], [float(v) for v in sine.coef]


def cos_sin_turns(turns):
    cosine, sine = unit_polys()
    frac = turns - jnp.round(turns)
    z = frac * frac

    def horner(coef):
        value = jnp.full_like(z, coef[-1])
        for v in coef[-2::-1]:
            value = value * z + v
        return value

    return horner(cosine), horner(sine) * frac


def azimuth_block(col, in_ref, slope_ref, centre_ref, fwd_ref, inv_ref, sel_ref, out_ref, keep):
    total = in_ref.shape[1]
    lead = total // LANES
    at = pl.ds(col, 2 * LANES)
    values = [
        tuple(in_ref[q, LANES * a : LANES * a + LANES, at].astype(f32) for q in range(2))
        for a in range(lead)
    ]
    values = fft_list(values, -1.0)
    sharp = slope_ref[:, at] * (total / 8.0)
    centre = centre_ref[:, at]
    back = []
    for c in range(lead):
        h, l = split(jnp.concatenate(values[c], axis=0))
        y = dot(fwd_ref[0, c], h) + dot(fwd_ref[0, c], l) + dot(fwd_ref[1, c], h)
        k = c + lead * lax.broadcasted_iota(jnp.int32, (LANES, 1), 0)
        u = jnp.where(k >= total // 2, k - total, k).astype(f32) * (1.0 / total)
        w = u - centre
        co, si = cos_sin_turns(sharp * w * w)
        re, im = y[:LANES], y[LANES:]
        h, l = split(jnp.concatenate([re * co - im * si, re * si + im * co], axis=0))
        y = dot(inv_ref[0, c], h) + dot(inv_ref[0, c], l) + dot(inv_ref[1, c], h)
        back.append((y[:LANES], y[LANES:]))
    half = PATCH // 2
    for a, pair in enumerate(fft_list(back, 1.0)):
        for q in range(2):
            image = pair[q].astype(bf16)
            out_ref[q, LANES * a : LANES * a + LANES, at] = image
            crop = dot(image[half : half + PATCH], sel_ref[...])
            keep(q, a, crop.astype(bf16))


def focus_body(
    names, sizes, valid_ref, root_ref, echo_ref, filt_ref, tw_ref, rf_ref, ri_ref,
    slope_ref, centre_ref, af_ref, ai_ref, sel_ref,
    image_ref, left_ref, right_ref, prime_ref,
    zh, zl, comp, turned, crop, pass_up, pass_down, from_up, from_down,
    send_sem, recv_sem, halo_send, halo_recv, up_send, up_recv, down_send, down_recv,
):
    here = {name: lax.axis_index(name) for name in names}
    me, peers = here["lines"], sizes["lines"]
    spot, stack_size = here["acq"], sizes["acq"]
    rows = echo_ref.shape[2]
    cols = image_ref.shape[2]
    block = min(rows, 32)
    blocks = rows // block
    wide = 2 * LANES
    parts = cols // wide

    def device(axis, index):
        return tuple(index if name == axis else here[name] for name in names)

    def remote(src, dst, send, recv, axis, index):
        return pltpu.make_async_remote_copy(
            src_ref=src, dst_ref=dst, send_sem=send, recv_sem=recv,
            device_id=device(axis, index), device_id_type=pl.DeviceIdType.MESH,
        )

    @pl.when(me == 0)
    def _():
        left_ref[...] = jnp.zeros_like(left_ref)

    @pl.when(me == peers - 1)
    def _():
        right_ref[...] = jnp.zeros_like(right_ref)

    @pl.when(spot == 0)
    def _():
        from_up[...] = jnp.zeros_like(from_up)

    @pl.when(spot == stack_size - 1)
    def _():
        from_down[...] = jnp.zeros_like(from_down)

    barrier = pltpu.get_barrier_semaphore()
    targets = [("lines", (me + d) % peers) for d in range(1, peers)]
    targets += [("acq", (spot + d) % stack_size) for d in (1, stack_size - 1)]
    for axis, index in targets:
        pl.semaphore_signal(
            barrier, inc=1, device_id=device(axis, index), device_id_type=pl.DeviceIdType.MESH
        )
    pl.semaphore_wait(barrier, len(targets))

    def exchange(d, b, j):
        to = (me + d) % peers
        source = pl.ds(pl.multiple_of(to * cols + j * wide, wide), wide)
        land = pl.ds(pl.multiple_of(me * rows + b * block, block), block)
        return remote(
            comp.at[:, pl.ds(pl.multiple_of(b * block, block), block), source],
            turned.at[:, land, pl.ds(pl.multiple_of(j * wide, wide), wide)],
            send_sem.at[d - 1, b, j], recv_sem.at[d - 1, b, j], "lines", to,
        )

    order = sorted(range(1, peers), key=lambda d: -min(d, peers - d))

    def send(b, j):
        for d in order:
            exchange(d, b, j).start()

    def compress(b, carry):
        r0 = pl.multiple_of(b * block, block)
        range_block(
            r0, block, me * rows, valid_ref[0], echo_ref, filt_ref, tw_ref, rf_ref, ri_ref,
            comp, zh, zl,
        )
        own = pl.ds(pl.multiple_of(me * cols, wide), cols)
        turned[:, pl.ds(pl.multiple_of(me * rows + r0, block), block), :] = comp[
            :, pl.ds(r0, block), own
        ]
        send(b, 0)

        @pl.when(b < blocks - 2)
        def _():
            lax.fori_loop(1, parts, lambda j, x: (send(b, j), x)[1], 0)

        return carry

    lax.fori_loop(0, blocks, compress, 0)

    def send_late(j, carry):
        for b in range(max(blocks - 2, 0), blocks):
            send(b, j)
        return carry

    lax.fori_loop(1, parts, send_late, 0)
    mine = root_ref[0] == spot

    def chain(at, last, buffer, staged, send_sems, recv_sems, step):
        ahead = spot + step
        return remote(
            staged.at[at], buffer.at[at], send_sems.at[at], recv_sems.at[at], "acq",
            (ahead + stack_size) % stack_size,
        )

    lanes = (
        (spot, spot == 0, spot == stack_size - 1, from_up, pass_up, up_send, up_recv, 1),
        (
            stack_size - 1 - spot, spot == stack_size - 1, spot == 0,
            from_down, pass_down, down_send, down_recv, -1,
        ),
    )

    def forward(tick):
        for depth, opening, ending, buffer, staged, sends, recvs, step in lanes:
            at = tick - depth

            @pl.when(jnp.logical_and(at >= 0, at < parts))
            def _():
                copy = chain(at, None, buffer, staged, sends, recvs, step)

                @pl.when(jnp.logical_not(opening))
                def _():
                    copy.wait_recv()

                @pl.when(jnp.logical_not(ending))
                def _():
                    staged[at] = jnp.where(mine, crop[at], buffer[at])
                    copy.start()

    tile = lambda ref, col: ref.at[:, :, col : col + LANES]
    to_left = remote(
        tile(image_ref, 0), right_ref, halo_send.at[0], halo_recv.at[0],
        "lines", (me + peers - 1) % peers,
    )
    to_right = remote(
        tile(image_ref, cols - LANES), left_ref, halo_send.at[1], halo_recv.at[1],
        "lines", (me + 1) % peers,
    )

    def focus(j, carry):
        for d in order:
            for b in range(blocks):
                exchange(d, b, j).wait_recv()

        def keep(q, a, value):
            crop[j, q, PATCH * a : PATCH * a + PATCH, :] = value

        azimuth_block(
            pl.multiple_of(j * wide, wide), turned, slope_ref, centre_ref, af_ref, ai_ref,
            sel_ref, image_ref, keep,
        )
        forward(j)
        return carry

    lax.fori_loop(0, parts, focus, 0)

    @pl.when(me > 0)
    def _():
        to_left.start()

    @pl.when(me < peers - 1)
    def _():
        to_right.start()

    lax.fori_loop(parts, parts + stack_size - 1, lambda t, x: (forward(t), x)[1], 0)
    for j in range(parts):
        prime_ref[:, :, LANES * j : LANES * j + LANES] = jnp.where(
            mine, crop[j], jnp.where(root_ref[0] < spot, from_up[j], from_down[j])
        )

    @pl.when(me > 0)
    def _():
        to_left.wait_send()
        to_right.wait_recv()

    @pl.when(me < peers - 1)
    def _():
        to_right.wait_send()
        to_left.wait_recv()

    for depth, opening, ending, buffer, staged, sends, recvs, step in lanes:

        @pl.when(jnp.logical_not(ending))
        def _():
            for j in range(parts):
                chain(j, None, buffer, staged, sends, recvs, step).wait_send()

    def finish(j, carry):
        for d in order:
            for b in range(blocks):
                exchange(d, b, j).wait_send()
        return carry

    lax.fori_loop(0, parts, finish, 0)


def focus(names, sizes, valid, root, echo, filt, slope, centre):
    rows, length = echo.shape[2:]
    lead = length // LANES
    block = min(rows, 32)
    blocks = rows // block
    total, cols = rows * sizes["lines"], slope.shape[1]
    peers = sizes["lines"] - 1
    wide = 2 * LANES
    parts = cols // wide
    rf = halves(right_form(dft(LANES, -1.0)))
    ri = halves(right_form(dft(LANES, 1.0)))
    angle = 2 * np.pi * np.outer(np.arange(lead), np.arange(LANES)) / length
    tw = np.stack([np.cos(angle), -np.sin(angle)]).astype(np.float32)
    filt = filt[0].reshape(2, LANES, lead).transpose(0, 2, 1) * (1.0 / length)
    fwd, inv = [], []
    for c in range(total // LANES):
        phase = np.exp(-2j * np.pi * c * np.arange(LANES) / total)
        fwd.append(left_form(dft(LANES, -1.0) * phase[None, :]))
        inv.append(left_form(dft(LANES, 1.0) * phase.conj()[:, None] / total))
    fwd, inv = halves(np.stack(fwd)), halves(np.stack(inv))
    sel = np.zeros((wide, LANES), np.float32)
    lane = np.arange(PATCH)
    sel[lane + PATCH // 2, lane] = 1
    sel[lane + LANES + PATCH // 2, lane + PATCH] = 1
    sel = sel.astype(bf16)
    smem, vmem = pl.BlockSpec(memory_space=pltpu.SMEM), pl.BlockSpec(memory_space=pltpu.VMEM)
    dma = pltpu.SemaphoreType.DMA
    chunk = pltpu.VMEM((parts, 2, total // 2, LANES), bf16)
    return pl.pallas_call(
        functools.partial(focus_body, names, sizes),
        in_specs=[smem] * 2 + [vmem] * 10,
        out_specs=[vmem] * 4,
        out_shape=[
            jax.ShapeDtypeStruct((2, total, cols), bf16),
            jax.ShapeDtypeStruct((2, total, LANES), bf16),
            jax.ShapeDtypeStruct((2, total, LANES), bf16),
            jax.ShapeDtypeStruct((2, total // 2, cols // 2), bf16),
        ],
        scratch_shapes=[
            pltpu.VMEM((lead * block, wide), bf16),
            pltpu.VMEM((lead * block, wide), bf16),
            pltpu.VMEM((2, rows, length), bf16),
            pltpu.VMEM((2, total, cols), bf16),
        ]
        + [chunk] * 5
        + [dma((peers, blocks, parts))] * 2
        + [dma((2,))] * 2
        + [dma((parts,))] * 4,
        compiler_params=pltpu.CompilerParams(collective_id=0, has_side_effects=True),
        name="focus",
    )(valid, root, echo, filt, tw, rf, ri, slope, centre, fwd, inv, sel)


def correlate_body(
    off_ref, image_ref, left_ref, right_ref, crop_ref, fr_ref, fl_ref, ir_ref, il_ref, ones_ref,
    out_ref, padded, stack, high, low, power,
):
    total, cols = image_ref.shape[1:]
    half = PATCH // 2
    row_blocks, pairs = total // LANES, cols // (2 * LANES)
    count = row_blocks * pairs
    for q in range(2):
        padded[q, :half, :] = jnp.zeros((half, cols + 3 * LANES), f32)
        padded[q, half + total :, :] = jnp.zeros((half + 8, cols + 3 * LANES), f32)
        padded[q, half : half + total, :LANES] = left_ref[q].astype(f32)
        padded[q, half : half + total, LANES : LANES + cols] = image_ref[q].astype(f32)
        padded[q, half : half + total, LANES + cols : 2 * LANES + cols] = right_ref[q].astype(f32)
    lane = lax.broadcasted_iota(jnp.int32, (1, LANES), 1)

    def window(q, i, j, target):
        row = LANES * i + PATCH + off_ref[0, 0, i, j]
        col = LANES * j + LANES + half + off_ref[0, 1, i, j]
        base = pl.multiple_of(col // LANES * LANES, LANES)
        offset = col - base
        shift = (target - offset + LANES) % LANES
        top = pl.multiple_of(row // 8 * 8, 8)
        first = padded[q, pl.ds(top, PATCH + 8), pl.ds(base, LANES)]
        second = padded[q, pl.ds(top, PATCH + 8), pl.ds(pl.multiple_of(base + LANES, LANES), LANES)]
        first = pltpu.roll(first, shift, 1)
        second = pltpu.roll(second, shift, 1)
        joined = jnp.where(lane + offset - target < LANES, first, second)
        return pltpu.roll(joined, (PATCH + 8 - (row - top)) % (PATCH + 8), 0)[:PATCH]

    def total_of(re, im):
        return jnp.sum(re * re + im * im, axis=0, keepdims=True)

    for i in range(row_blocks):
        for jp in range(pairs):
            n = i * pairs + jp
            parts = [
                jnp.where(lane < PATCH, window(q, i, 2 * jp, 0), window(q, i, 2 * jp + 1, PATCH))
                for q in range(2)
            ]
            power[count + n : count + n + 1, :] = total_of(*parts)
            prime = [
                crop_ref[q, PATCH * i : PATCH * i + PATCH, LANES * jp : LANES * jp + LANES]
                for q in range(2)
            ]
            power[n : n + 1, :] = total_of(prime[0].astype(f32), prime[1].astype(f32))
            for q in range(2):
                stack[PATCH * n : PATCH * n + PATCH, LANES * q : LANES * q + LANES] = prime[q]
                at = PATCH * (count + n)
                stack[at : at + PATCH, LANES * q : LANES * q + LANES] = parts[q].astype(bf16)

    y = dot(stack[...], fr_ref[0]) + dot(stack[...], fr_ref[1])
    for n in range(2 * count):
        part = y[PATCH * n : PATCH * n + PATCH]
        for q in range(2):
            h, l = split(part[:, LANES * q : LANES * q + LANES])
            high[PATCH * q : PATCH * q + PATCH, LANES * n : LANES * n + LANES] = h
            low[PATCH * q : PATCH * q + PATCH, LANES * n : LANES * n + LANES] = l

    def left(m_ref, h, l):
        return dot(m_ref[0], h) + dot(m_ref[0], l) + dot(m_ref[1], h)

    z = left(fl_ref, high[...], low[...])
    wide = count * LANES
    pr, pi, sr, si = z[:PATCH, :wide], z[PATCH:, :wide], z[:PATCH, wide:], z[PATCH:, wide:]
    cross = jnp.concatenate([pr * sr + pi * si, pi * sr - pr * si], axis=0)
    x = left(il_ref, *split(cross))
    for n in range(count):
        for q in range(2):
            h, l = split(x[PATCH * q : PATCH * q + PATCH, LANES * n : LANES * n + LANES])
            stack[PATCH * n : PATCH * n + PATCH, LANES * q : LANES * q + LANES] = h
            at = PATCH * (count + n)
            stack[at : at + PATCH, LANES * q : LANES * q + LANES] = l
    h, l = stack[: PATCH * count], stack[PATCH * count :]
    y = dot(h, ir_ref[0]) + dot(l, ir_ref[0]) + dot(h, ir_ref[1])
    means = jnp.dot(
        power[...], ones_ref[...], precision=lax.Precision.HIGHEST, preferred_element_type=f32
    )
    scale = lax.rsqrt(means + eps)
    factor = scale[:count] * scale[count:] * (1.0 / PATCH**3)
    for i in range(row_blocks):
        for jp in range(pairs):
            n = i * pairs + jp
            part = y[PATCH * n : PATCH * n + PATCH]
            for q in range(2):
                out_ref[
                    0, q, PATCH * i : PATCH * i + PATCH, LANES * jp : LANES * jp + LANES
                ] = part[:, LANES * q : LANES * q + LANES] * factor[n : n + 1, :]


def correlate(offsets, image, left, right, crop):
    total, cols = image.shape[1:]
    count = (total // LANES) * (cols // (2 * LANES))
    two = np.eye(2)
    fr = halves(right_form(np.kron(two, dft(PATCH, -1.0))))
    ir = halves(right_form(np.kron(two, dft(PATCH, 1.0))))
    fl = halves(left_form(dft(PATCH, -1.0)))
    il = halves(left_form(dft(PATCH, 1.0)))
    ones = np.kron(two, np.full((PATCH, PATCH), 1.0 / PATCH**2)).astype(np.float32)
    vmem = pl.BlockSpec(memory_space=pltpu.VMEM)
    return pl.pallas_call(
        correlate_body,
        in_specs=[pl.BlockSpec(memory_space=pltpu.SMEM)] + [vmem] * 9,
        out_specs=vmem,
        out_shape=jax.ShapeDtypeStruct((1, 2, total // 2, cols // 2), f32),
        scratch_shapes=[
            pltpu.VMEM((2, total + PATCH + 8, cols + 3 * LANES), f32),
            pltpu.VMEM((2 * count * PATCH, 2 * LANES), bf16),
            pltpu.VMEM((2 * PATCH, 2 * count * LANES), bf16),
            pltpu.VMEM((2 * PATCH, 2 * count * LANES), bf16),
            pltpu.VMEM((2 * count, LANES), f32),
        ],
        name="correlate",
    )(offsets, image, left, right, crop, fr, fl, ir, il, ones)


def on_device(names, sizes, echo, filt, slope, centre, valid, reference_index, offsets):
    image, left, right, primary = focus(
        names, sizes, valid, reference_index, echo, filt, slope, centre
    )
    return correlate(offsets, image, left, right, primary)


def solution(mesh):
    names = tuple(mesh.axis_names)
    sizes = {name: int(mesh.shape[name]) for name in names}
    return jax.shard_map(
        functools.partial(on_device, names, sizes),
        mesh=mesh,
        in_specs=(
            P(("stack", "acq"), None, "lines", None),
            P(("stack", "acq"), None, None),
            P(("stack", "acq"), "lines"),
            P(("stack", "acq"), "lines"),
            P(("stack", "acq")),
            P("stack"),
            P(("stack", "acq"), None, None, "lines"),
        ),
        out_specs=P(("stack", "acq"), None, None, "lines"),
        check_vma=False,
    )
```

```python
import functools
import math

import jax
import jax.numpy as jnp
import numpy as np
from jax import lax
from jax.experimental import pallas as pl
from jax.experimental.pallas import tpu as pltpu
from jax.sharding import PartitionSpec as P

PATCH = 64
LANES = 128
eps = 1e-06
bf16 = jnp.bfloat16
f32 = jnp.float32


def dft(size, sign):
    index = np.arange(size)
    angle = 2.0 * np.pi * (np.outer(index, index) % size) / size
    return np.cos(angle) + 1j * sign * np.sin(angle)


def right_form(matrix):
    return np.block([[matrix.real, matrix.imag], [-matrix.imag, matrix.real]])


def left_form(matrix):
    return np.block([[matrix.real, -matrix.imag], [matrix.imag, matrix.real]])


def halves(matrix):
    high = np.asarray(matrix, np.float32).astype(bf16)
    low = (np.asarray(matrix, np.float64) - high.astype(np.float64)).astype(bf16)
    return np.stack([high, low])


def split(value):
    high = value.astype(bf16)
    return high, (value - high.astype(f32)).astype(bf16)


def dot(a, b):
    return jnp.dot(a, b, preferred_element_type=f32)


def dot_nt(a, b):
    return lax.dot_general(a, b, (((1,), (1,)), ((), ())), preferred_element_type=f32)


def dot_tn(a, b):
    return lax.dot_general(a, b, (((0,), (0,)), ((), ())), preferred_element_type=f32)


def fft_list(values, sign):
    count = len(values)
    if count == 1:
        return values
    even = fft_list(values[0::2], sign)
    odd = fft_list(values[1::2], sign)
    out = [None] * count
    for k in range(count // 2):
        re, im = odd[k]
        if k == 0:
            pass
        elif 4 * k == count:
            re, im = (-im, re) if sign > 0 else (im, -re)
        elif 8 * k == count:
            r = math.sqrt(0.5)
            re, im = ((re - im) * r, (re + im) * r) if sign > 0 else ((re + im) * r, (im - re) * r)
        elif 8 * k == 3 * count:
            r = math.sqrt(0.5)
            re, im = ((re + im) * -r, (re - im) * r) if sign > 0 else ((im - re) * r, (re + im) * -r)
        else:
            c = math.cos(2 * math.pi * k / count)
            s = sign * math.sin(2 * math.pi * k / count)
            re, im = re * c - im * s, re * s + im * c
        out[k] = (even[k][0] + re, even[k][1] + im)
        out[k + count // 2] = (even[k][0] - re, even[k][1] - im)
    return out


def range_block(r0, block, first, valid, echo_ref, filt_ref, tw_ref, fwd_ref, out_ref, zh, zl):
    lead = echo_ref.shape[3] // LANES
    group = 16

    def put(row, count, re, im):
        zh[row : row + count, :LANES], zl[row : row + count, :LANES] = split(re)
        zh[row : row + count, LANES:], zl[row : row + count, LANES:] = split(im)

    def product(mul):
        h = zh[...]
        return mul(h, fwd_ref[0]) + mul(zl[...], fwd_ref[0]) + mul(h, fwd_ref[1])

    for g in range(block // group):
        at = pl.multiple_of(r0 + g * group, group)
        line = first + at + lax.broadcasted_iota(jnp.int32, (group, 1), 0)
        keep = (line < valid).astype(f32)
        values = [
            tuple(
                echo_ref[0, q, pl.ds(at, group), LANES * a : LANES * a + LANES].astype(f32) * keep
                for q in range(2)
            )
            for a in range(lead)
        ]
        for c, (re, im) in enumerate(fft_list(values, -1.0)):
            tr, ti = tw_ref[0, c : c + 1, :], tw_ref[1, c : c + 1, :]
            put(c * block + g * group, group, re * tr - im * ti, re * ti + im * tr)
    y = product(dot)
    for c in range(lead):
        part = y[c * block : c * block + block]
        re, im = part[:, :LANES], part[:, LANES:]
        hr, hi = filt_ref[0, c : c + 1, :], filt_ref[1, c : c + 1, :]
        put(c * block, block, re * hr - im * hi, re * hi + im * hr)
    y = product(dot_nt)
    for g in range(block // group):
        at = pl.multiple_of(r0 + g * group, group)
        values = []
        for c in range(lead):
            part = y[c * block + g * group : c * block + g * group + group]
            re, im = part[:, :LANES], part[:, LANES:]
            tr, ti = tw_ref[0, c : c + 1, :], tw_ref[1, c : c + 1, :]
            values.append((re * tr + im * ti, im * tr - re * ti))
        for a, pair in enumerate(fft_list(values, 1.0)):
            for q in range(2):
                out_ref[q, pl.ds(at, group), LANES * a : LANES * a + LANES] = pair[q].astype(bf16)


def unit_polys():
    z = 0.125 - 0.125 * np.cos(np.pi * (np.arange(400) + 0.5) / 400)
    f = np.sqrt(z)
    cosine = np.polynomial.Polynomial.fit(z, np.cos(2 * np.pi * f), 7, domain=[0, 0.25]).convert()
    sine = np.polynomial.Polynomial.fit(z, np.sin(2 * np.pi * f) / f, 6, domain=[0, 0.25]).convert()
    return [float(v) for v in cosine.coef], [float(v) for v in sine.coef]


def cos_sin_turns(turns):
    cosine, sine = unit_polys()
    frac = turns - jnp.round(turns)
    z = frac * frac

    def horner(coef):
        value = jnp.full_like(z, coef[-1])
        for v in coef[-2::-1]:
            value = value * z + v
        return value

    return horner(cosine), horner(sine) * frac


def azimuth_block(col, in_ref, slope_ref, centre_ref, fwd_ref, sel_ref, out_ref, keep):
    total = in_ref.shape[1]
    lead = total // LANES
    at = pl.ds(col, 2 * LANES)
    values = [
        tuple(in_ref[q, LANES * a : LANES * a + LANES, at].astype(f32) for q in range(2))
        for a in range(lead)
    ]
    values = fft_list(values, -1.0)
    sharp = slope_ref[:, at] * (total / 8.0)
    centre = centre_ref[:, at]
    back = []
    for c in range(lead):
        h, l = split(jnp.concatenate(values[c], axis=0))
        y = dot(fwd_ref[0, c], h) + dot(fwd_ref[0, c], l) + dot(fwd_ref[1, c], h)
        k = c + lead * lax.broadcasted_iota(jnp.int32, (LANES, 1), 0)
        u = jnp.where(k >= total // 2, k - total, k).astype(f32) * (1.0 / total)
        w = u - centre
        co, si = cos_sin_turns(sharp * w * w)
        re, im = y[:LANES], y[LANES:]
        h, l = split(jnp.concatenate([re * co - im * si, re * si + im * co], axis=0))
        y = dot_tn(fwd_ref[0, c], h) + dot_tn(fwd_ref[0, c], l) + dot_tn(fwd_ref[1, c], h)
        y = y * (1.0 / total)
        back.append((y[:LANES], y[LANES:]))
    half = PATCH // 2
    for a, pair in enumerate(fft_list(back, 1.0)):
        for q in range(2):
            image = pair[q].astype(bf16)
            out_ref[q, LANES * a : LANES * a + LANES, at] = image
            crop = dot(image[half : half + PATCH], sel_ref[...])
            keep(q, a, crop.astype(bf16))


def focus_body(
    names, sizes, valid_ref, root_ref, echo_ref, filt_ref, tw_ref, rf_ref,
    slope_ref, centre_ref, af_ref, sel_ref, off_ref, fr_ref, fl_ref, il_ref, ones_ref,
    out_ref, image_ref, left_ref, right_ref, padded, stack, power,
    zh, zl, comp, turned, crop, pass_up, pass_down, from_up, from_down,
    send_sem, recv_sem, halo_send, halo_recv, up_send, up_recv, down_send, down_recv,
):
    here = {name: lax.axis_index(name) for name in names}
    me, peers = here["lines"], sizes["lines"]
    spot, stack_size = here["acq"], sizes["acq"]
    rows = echo_ref.shape[2]
    cols = image_ref.shape[2]
    block = min(rows, 32)
    blocks = rows // block
    wide = 2 * LANES
    parts = cols // wide

    def device(axis, index):
        return tuple(index if name == axis else here[name] for name in names)

    def remote(src, dst, send, recv, axis, index):
        return pltpu.make_async_remote_copy(
            src_ref=src, dst_ref=dst, send_sem=send, recv_sem=recv,
            device_id=device(axis, index), device_id_type=pl.DeviceIdType.MESH,
        )

    @pl.when(me == 0)
    def _():
        left_ref[...] = jnp.zeros_like(left_ref)

    @pl.when(me == peers - 1)
    def _():
        right_ref[...] = jnp.zeros_like(right_ref)

    @pl.when(spot == 0)
    def _():
        from_up[...] = jnp.zeros_like(from_up)

    @pl.when(spot == stack_size - 1)
    def _():
        from_down[...] = jnp.zeros_like(from_down)

    barrier = pltpu.get_barrier_semaphore()
    targets = [("lines", (me + d) % peers) for d in range(1, peers)]
    targets += [("acq", (spot + d) % stack_size) for d in (1, stack_size - 1)]
    for axis, index in targets:
        pl.semaphore_signal(
            barrier, inc=1, device_id=device(axis, index), device_id_type=pl.DeviceIdType.MESH
        )
    pl.semaphore_wait(barrier, len(targets))

    def exchange(d, b, j):
        to = (me + d) % peers
        source = pl.ds(pl.multiple_of(to * cols + j * wide, wide), wide)
        land = pl.ds(pl.multiple_of(me * rows + b * block, block), block)
        return remote(
            comp.at[:, pl.ds(pl.multiple_of(b * block, block), block), source],
            turned.at[:, land, pl.ds(pl.multiple_of(j * wide, wide), wide)],
            send_sem.at[d - 1, b, j], recv_sem.at[d - 1, b, j], "lines", to,
        )

    order = sorted(range(1, peers), key=lambda d: -min(d, peers - d))

    def send(b, j):
        for d in order:
            exchange(d, b, j).start()

    def compress(b, carry):
        r0 = pl.multiple_of(b * block, block)
        range_block(
            r0, block, me * rows, valid_ref[0], echo_ref, filt_ref, tw_ref, rf_ref,
            comp, zh, zl,
        )
        own = pl.ds(pl.multiple_of(me * cols, wide), cols)
        turned[:, pl.ds(pl.multiple_of(me * rows + r0, block), block), :] = comp[
            :, pl.ds(r0, block), own
        ]
        send(b, 0)

        @pl.when(b < blocks - 2)
        def _():
            lax.fori_loop(1, parts, lambda j, x: (send(b, j), x)[1], 0)

        return carry

    lax.fori_loop(0, blocks, compress, 0)

    def send_late(j, carry):
        for b in range(max(blocks - 2, 0), blocks):
            send(b, j)
        return carry

    lax.fori_loop(1, parts, send_late, 0)
    mine = root_ref[0] == spot

    def chain(at, last, buffer, staged, send_sems, recv_sems, step):
        ahead = spot + step
        return remote(
            staged.at[at], buffer.at[at], send_sems.at[at], recv_sems.at[at], "acq",
            (ahead + stack_size) % stack_size,
        )

    lanes = (
        (spot, spot == 0, spot == stack_size - 1, from_up, pass_up, up_send, up_recv, 1),
        (
            stack_size - 1 - spot, spot == stack_size - 1, spot == 0,
            from_down, pass_down, down_send, down_recv, -1,
        ),
    )

    def forward(tick):
        for depth, opening, ending, buffer, staged, sends, recvs, step in lanes:
            at = tick - depth

            @pl.when(jnp.logical_and(at >= 0, at < parts))
            def _():
                copy = chain(at, None, buffer, staged, sends, recvs, step)

                @pl.when(jnp.logical_not(opening))
                def _():
                    copy.wait_recv()

                @pl.when(jnp.logical_not(ending))
                def _():
                    staged[at] = jnp.where(mine, crop[at], buffer[at])
                    copy.start()

    tile = lambda ref, col: ref.at[:, :, col : col + LANES]
    to_left = remote(
        tile(image_ref, 0), right_ref, halo_send.at[0], halo_recv.at[0],
        "lines", (me + peers - 1) % peers,
    )
    to_right = remote(
        tile(image_ref, cols - LANES), left_ref, halo_send.at[1], halo_recv.at[1],
        "lines", (me + 1) % peers,
    )

    def focus(j, carry):
        for d in order:
            for b in range(blocks):
                exchange(d, b, j).wait_recv()

        def keep(q, a, value):
            crop[j, q, PATCH * a : PATCH * a + PATCH, :] = value

        azimuth_block(
            pl.multiple_of(j * wide, wide), turned, slope_ref, centre_ref, af_ref,
            sel_ref, image_ref, keep,
        )
        forward(j)

        @pl.when(jnp.logical_and(j == 0, me > 0))
        def _():
            to_left.start()

        return carry

    lax.fori_loop(0, parts, focus, 0)

    @pl.when(me < peers - 1)
    def _():
        to_right.start()

    total = image_ref.shape[1]
    half = PATCH // 2
    row_blocks = total // LANES
    count = row_blocks * parts
    def pad():
        for q in range(2):
            padded[q, :half, :] = jnp.zeros((half, cols + 2 * LANES), bf16)
            padded[q, half + total :, :] = jnp.zeros((half, cols + 2 * LANES), bf16)
            padded[q, half : half + total, LANES : LANES + cols] = image_ref[q]

    def one_hot(condition):
        return jnp.where(condition, 1.0, 0.0).astype(bf16)

    def pair_window(i, jp):
        base = pl.multiple_of(LANES * i, LANES)
        picked, places = [], []
        for s in range(2):
            j = 2 * jp + s
            row = PATCH + off_ref[0, 0, i, j]
            col = LANES + half + off_ref[0, 1, i, j] - PATCH * s
            m = lax.broadcasted_iota(jnp.int32, (PATCH, 3 * PATCH), 0)
            r = lax.broadcasted_iota(jnp.int32, (PATCH, 3 * PATCH), 1)
            rows_of = one_hot(r - m == row)
            picked.append(jnp.concatenate([
                dot(
                    rows_of,
                    padded[q, pl.ds(base, 3 * PATCH), LANES * j : LANES * j + 3 * LANES],
                ).astype(bf16)
                for q in range(2)
            ], axis=0))
            c = lax.broadcasted_iota(jnp.int32, (3 * LANES, LANES), 0)
            n = lax.broadcasted_iota(jnp.int32, (3 * LANES, LANES), 1)
            side = (n < PATCH) if s == 0 else (n >= PATCH)
            places.append(one_hot(jnp.logical_and(c - n == col, side)))
        both = dot(picked[0], places[0]) + dot(picked[1], places[1])
        return both[:PATCH], both[PATCH:]

    def put(n, pair):
        at = pl.ds(pl.multiple_of(PATCH * n, PATCH), PATCH)
        for q in range(2):
            stack[at, LANES * q : LANES * q + LANES] = pair[q].astype(bf16)
        re, im = pair[0].astype(f32), pair[1].astype(f32)
        power[pl.ds(n, 1), :] = jnp.sum(re * re + im * im, axis=0, keepdims=True)

    def windows():
        @pl.when(me > 0)
        def _():
            to_left.wait_send()
            to_right.wait_recv()

        @pl.when(me < peers - 1)
        def _():
            to_right.wait_send()
            to_left.wait_recv()

        for q in range(2):
            padded[q, half : half + total, :LANES] = left_ref[q]
            padded[q, half : half + total, LANES + cols :] = right_ref[q]

        def row_of(i, carry):
            for jp in range(parts):
                pair = pair_window(i, jp)
                put(count + i * parts + jp, pair)
            return carry

        lax.fori_loop(0, row_blocks, row_of, 0)

    def left(m_ref, value):
        h, l = split(value)
        return dot(m_ref[0], h) + dot(m_ref[0], l) + dot(m_ref[1], h)

    def spectrum(start):
        data = stack[PATCH * start : PATCH * (start + count)]
        y = dot(data, fr_ref[0]) + dot(data, fr_ref[1])
        return left(fl_ref, jnp.concatenate([
            jnp.concatenate(
                [y[PATCH * n : PATCH * n + PATCH, LANES * q : LANES * q + LANES] for n in range(count)],
                axis=1,
            )
            for q in range(2)
        ], axis=0))

    work = [pad, windows]
    for tick in range(stack_size - 1):
        forward(parts + tick)
        if work:
            work.pop(0)()
    for step in work:
        step()
    z = spectrum(count)
    sr, si = z[:PATCH], z[PATCH:]
    for i in range(row_blocks):
        for jp in range(parts):
            at = slice(PATCH * i, PATCH * i + PATCH)
            put(i * parts + jp, [
                jnp.where(
                    mine, crop[jp, q, at],
                    jnp.where(root_ref[0] < spot, from_up[jp, q, at], from_down[jp, q, at]),
                )
                for q in range(2)
            ])
    z = spectrum(0)
    pr, pi = z[:PATCH], z[PATCH:]
    x = left(il_ref, jnp.concatenate([pr * sr + pi * si, pi * sr - pr * si], axis=0))
    x = jnp.concatenate([
        jnp.concatenate(
            [x[PATCH * q : PATCH * q + PATCH, LANES * n : LANES * n + LANES] for n in range(count)],
            axis=0,
        )
        for q in range(2)
    ], axis=1)
    h, l = split(x)
    y = dot_nt(h, fr_ref[0]) + dot_nt(l, fr_ref[0]) + dot_nt(h, fr_ref[1])
    means = jnp.dot(
        power[...], ones_ref[...], precision=lax.Precision.HIGHEST, preferred_element_type=f32
    )
    scale = lax.rsqrt(means + eps)
    factor = scale[:count] * scale[count:] * (1.0 / PATCH**3)
    for i in range(row_blocks):
        for jp in range(parts):
            n = i * parts + jp
            part = y[PATCH * n : PATCH * n + PATCH]
            for q in range(2):
                out_ref[
                    0, q, PATCH * i : PATCH * i + PATCH, LANES * jp : LANES * jp + LANES
                ] = part[:, LANES * q : LANES * q + LANES] * factor[n : n + 1, :]

    for depth, opening, ending, buffer, staged, sends, recvs, step in lanes:

        @pl.when(jnp.logical_not(ending))
        def _():
            for j in range(parts):
                chain(j, None, buffer, staged, sends, recvs, step).wait_send()

    def finish(j, carry):
        for d in order:
            for b in range(blocks):
                exchange(d, b, j).wait_send()
        return carry

    lax.fori_loop(0, parts, finish, 0)


def focus(names, sizes, valid, root, echo, filt, slope, centre, offsets):
    rows, length = echo.shape[2:]
    lead = length // LANES
    block = min(rows, 32)
    blocks = rows // block
    total, cols = rows * sizes["lines"], slope.shape[1]
    peers = sizes["lines"] - 1
    wide = 2 * LANES
    parts = cols // wide
    rf = halves(right_form(dft(LANES, -1.0)))
    angle = 2 * np.pi * np.outer(np.arange(lead), np.arange(LANES)) / length
    tw = np.stack([np.cos(angle), -np.sin(angle)]).astype(np.float32)
    filt = filt[0].reshape(2, LANES, lead).transpose(0, 2, 1) * (1.0 / length)
    fwd = []
    for c in range(total // LANES):
        phase = np.exp(-2j * np.pi * c * np.arange(LANES) / total)
        fwd.append(left_form(dft(LANES, -1.0) * phase[None, :]))
    fwd = halves(np.stack(fwd))
    sel = np.zeros((wide, LANES), np.float32)
    lane = np.arange(PATCH)
    sel[lane + PATCH // 2, lane] = 1
    sel[lane + LANES + PATCH // 2, lane + PATCH] = 1
    sel = sel.astype(bf16)
    count = (total // LANES) * parts
    two = np.eye(2)
    fr = halves(right_form(np.kron(two, dft(PATCH, -1.0))))
    fl = halves(left_form(dft(PATCH, -1.0)))
    il = halves(left_form(dft(PATCH, 1.0)))
    ones = np.kron(two, np.full((PATCH, PATCH), 1.0 / PATCH**2)).astype(np.float32)
    smem, vmem = pl.BlockSpec(memory_space=pltpu.SMEM), pl.BlockSpec(memory_space=pltpu.VMEM)
    dma = pltpu.SemaphoreType.DMA
    chunk = pltpu.VMEM((parts, 2, total // 2, LANES), bf16)
    return pl.pallas_call(
        functools.partial(focus_body, names, sizes),
        in_specs=[smem] * 2 + [vmem] * 8 + [smem] + [vmem] * 4,
        out_specs=vmem,
        out_shape=jax.ShapeDtypeStruct((1, 2, total // 2, cols // 2), f32),
        scratch_shapes=[
            pltpu.VMEM((2, total, cols), bf16),
            pltpu.VMEM((2, total, LANES), bf16),
            pltpu.VMEM((2, total, LANES), bf16),
            pltpu.VMEM((2, total + PATCH, cols + 2 * LANES), bf16),
            pltpu.VMEM((2 * count * PATCH, 2 * LANES), bf16),
            pltpu.VMEM((2 * count, LANES), f32),
            pltpu.VMEM((lead * block, wide), bf16),
            pltpu.VMEM((lead * block, wide), bf16),
            pltpu.VMEM((2, rows, length), bf16),
            pltpu.VMEM((2, total, cols), bf16),
        ]
        + [chunk] * 5
        + [dma((peers, blocks, parts))] * 2
        + [dma((2,))] * 2
        + [dma((parts,))] * 4,
        compiler_params=pltpu.CompilerParams(collective_id=0, has_side_effects=True),
        name="focus",
    )(valid, root, echo, filt, tw, rf, slope, centre, fwd, sel, offsets, fr, fl, il, ones)


def on_device(names, sizes, echo, filt, slope, centre, valid, reference_index, offsets):
    return focus(names, sizes, valid, reference_index, echo, filt, slope, centre, offsets)


def solution(mesh):
    names = tuple(mesh.axis_names)
    sizes = {name: int(mesh.shape[name]) for name in names}
    return jax.shard_map(
        functools.partial(on_device, names, sizes),
        mesh=mesh,
        in_specs=(
            P(("stack", "acq"), None, "lines", None),
            P(("stack", "acq"), None, None),
            P(("stack", "acq"), "lines"),
            P(("stack", "acq"), "lines"),
            P(("stack", "acq")),
            P("stack"),
            P(("stack", "acq"), None, None, "lines"),
        ),
        out_specs=P(("stack", "acq"), None, None, "lines"),
        check_vma=False,
    )
```
